32 devices in a mesh: dp: 4 (over z), expert: 4 (over y, x), tensor: 2 (over core).
Axes of the slice: x: 2, y: 2, z: 4, core: 2. Of those that a mesh axis runs over, the one named last changes fastest.
Arguments:
- tokens: bfloat16 [512, 6144], P('dp'), may hold values from -6 to 6
- norm_gain: float32 [6144], replicated, may hold values from 0.1 to 1.9
- expert_ids: int32 [512, 2], P('dp'), may hold values from 0 to 3, all different within a row; in each aligned block of 128 rows (0 to 127, 128 to 255, ...) at most 72 rows name the same one
- gate_weights: float32 [512, 2], P('dp'), may hold values from 0.1 to 0.9
- w_gate: bfloat16 [4, 6144, 12288], P('expert', None, ('dp', 'tensor')), may hold values from -0.078125 to 0.078125
- w_up: bfloat16 [4, 6144, 12288], P('expert', None, ('dp', 'tensor')), may hold values from -0.078125 to 0.078125
- w_down: bfloat16 [4, 12288, 6144], P('expert', 'dp', 'tensor'), may hold values from -0.0546875 to 0.0546875
- label_rows: bfloat16 [512, 6144], P(('dp', 'expert'), 'tensor'), may hold values from -4 to 4, as said below
- seg_ids: int32 [4, 128], P('dp'), may hold values from 0 to 3, never falling along the last dimension, each value on 1 to 64 neighbouring positions
- pair_slot: int32 [4, 4], P('dp'), may hold values from 0 to 3, each once within a row
- ref_scores: float32 [4, 4], P('dp'), may hold values from -8 to 8
Outputs:
- layer_out: bfloat16 [512, 6144], P(('dp', 'expert'), 'tensor')
- margins: float32 [4, 2], P('dp')
The draws below stay inside these ranges and needn't reach their ends.
Inputs may be any that keep to these rules, and one draw needn't show every extreme that they name: `expert_ids`: each row names two different experts. Among the 128 rows of one dp group no expert is named more than 72 times, and in some group some expert is named exactly 72 times. `seg_ids`: within each row sequence numbers never fall; every sequence has 1 to 64 tokens and one has exactly 64. `pair_slot`: each row holds every number of 0 to 3 once. `label_rows`: entries lie within 27 / sqrt(6144) in magnitude.
All inputs are finite; a program needn't handle non-finite values.
Results may differ from the reference program's by a relative error of at most 0.009.
Values may be sent and summed in bfloat16 or wider, within the bound.
A program may use at most 128 MiB of HBM per device.

```python
import math
from functools import partial
import jax
import jax.numpy as jnp
import numpy as np
from jax import lax

D = 6144
FF = 12288
EXPERTS = 4
TOK_GROUP = 128
CAP = 72
TOKENS = 512
DPG = 4
SEQS = 4
PAIRS = 2
SEQ_MOST = 64
N_DP = 4


def draw_label_rows(key, part):
    row_pos = jnp.arange(TOKENS, dtype=jnp.float32)
    col_pos = jnp.arange(D, dtype=jnp.float32)
    row_rise = 1.0 + 2.0 * jnp.mod(row_pos, TOK_GROUP) / TOK_GROUP
    col_rise = 1.0 + 2.0 * col_pos / D
    base = jnp.clip(jax.random.normal(key, (TOKENS, D), jnp.float32), -6.0, 6.0)
    factor = 0.5 * row_rise[:, None] * col_rise[None, :]
    return (base * factor / math.sqrt(D)).astype(jnp.bfloat16)


def shard_levels(own_key, extent, cuts, least, high):
    loudness = 1.0
    for dim, parts in cuts:
        heights = jax.random.uniform(jax.random.fold_in(jax.random.fold_in(own_key, 6), dim), (parts,), jnp.float32, least / len(cuts), high / len(cuts))
        loudness = loudness * jnp.repeat(jnp.exp(heights), extent[dim] // parts).reshape((-1,) + (1,) * (len(extent) - 1 - dim))
    return loudness


def split_up(amount, total, most, slope):
    weights = [(1 << 20) // math.isqrt(standing ** slope) + 1 for standing in range(2, amount + 1)]
    rest, holding = total - most - (amount - 1), [1] * (amount - 1)
    while rest > 0:
        movable = [i for i in range(amount - 1) if holding[i] < most]
        mass, left = sum([weights[i] for i in movable]), rest
        for i in movable:
            extra = min(most - holding[i], max(1, left * weights[i] // mass), rest)
            holding[i] = holding[i] + extra
            rest = rest - extra
    return np.array([most] + holding)


def ragged_sizes(own_key, number_of, total, bound, slope):
    if number_of == 2:
        one = jax.random.randint(own_key, (), max(1, total - bound), min(bound, total - 1) + 1)
        return jnp.stack([one, total - one])
    tallies = jnp.asarray(split_up(number_of, total, bound, slope), jnp.int32)
    pairs = (number_of - 1) // 2
    giver, taker = tallies[1:1 + 2 * pairs:2], tallies[2:2 + 2 * pairs:2]
    margin = jnp.minimum(giver - 1, bound - taker)
    passed = jax.random.randint(jax.random.fold_in(own_key, 1), (pairs,), 0, 1 << 20) % (margin + 1)
    tallies = tallies.at[1:1 + 2 * pairs:2].set(giver - passed).at[2:2 + 2 * pairs:2].set(taker + passed)
    return tallies[jax.random.permutation(jax.random.fold_in(own_key, 2), number_of)]


def shared_out(key, own, number, rows, count, top, reach, slope):
    ranking = jax.random.permutation(key, count)
    heavy_load, common = shares(count, rows * top, reach, slope, True), shares(count, rows * top, reach, slope, False)
    places = jnp.arange(count)

    def named(tallies, rotation):
        used = int((tallies > 0).sum())
        fixed = max(1, used // 4)
        shifted = fixed + (places - fixed + rotation * (used - fixed)) % max(1, count - fixed)
        return jnp.zeros((count,), jnp.int32).at[ranking[jnp.where(places < fixed, places, shifted)]].set(jnp.asarray(tallies, jnp.int32))

    tallies = jnp.where(number % 4 == 0, named(heavy_load, number // 4), named(common, number - number // 4 - 1))
    mixed = jax.random.permutation(jax.random.fold_in(own, 3), count)
    source_of, receiver = mixed[0:count // 2 * 2:2], mixed[1:count // 2 * 2:2]
    room = jnp.minimum(tallies[source_of] - 1, reach - tallies[receiver]) // 2
    room = jnp.where((source_of == ranking[0]) | (receiver == ranking[0]) | (tallies[receiver] == 0), 0, jnp.maximum(room, 0))
    shifted = jax.random.randint(jax.random.fold_in(own, 4), (count // 2,), 0, 1 << 20) % (room + 1)
    tallies = tallies.at[source_of].add(-shifted).at[receiver].add(shifted)
    labels = jnp.searchsorted(jnp.cumsum(tallies), jnp.arange(rows * top), side="right").astype(jnp.int32)
    table = labels.reshape(top, rows).T
    table = table[jax.random.permutation(jax.random.fold_in(own, 1), rows)]
    rotation = jax.random.randint(jax.random.fold_in(own, 2), (rows, 1), 0, top)
    return jnp.take_along_axis(table, (jnp.arange(top)[None, :] + rotation) % top, axis=1)


def shares(number_of, total, limit, lean, full):
    weights = [(1 << 20) // math.isqrt(grade ** lean) + 1 for grade in range(1, number_of + 1)]
    largest = limit if full else min(limit, max(-(-total // number_of), total * weights[0] // sum(weights)))
    least = 1 if total - largest >= number_of - 1 else 0
    holding, rest = [largest] + [least] * (number_of - 1), total - largest - least * (number_of - 1)
    while rest > 0:
        candidates = [i for i in range(1, number_of) if holding[i] < largest] or [i for i in range(1, number_of) if holding[i] < limit]
        mass, left = sum([weights[i] for i in candidates]), rest
        for i in candidates:
            more = min(limit - holding[i], max(1, left * weights[i] // mass), rest)
            holding[i] = holding[i] + more
            rest = rest - more
    return np.array(holding)


def bell_draw(key, shape, width, reach, split=(), held_as=jnp.bfloat16):
    result = width * jax.random.normal(key, shape, jnp.float32)
    if split:
        result = result * shard_levels(key, shape, split, -0.22, 0.18)
    return jnp.clip(result, -reach, reach).astype(held_as)


def setup_inputs(seed: int = 0) -> dict:
    keys = jax.random.split(jax.random.key(seed), 12)
    tokens = bell_draw(keys[0], (TOKENS, D), 1.0, 6.0, ((0, 4),))
    norm_gain = jnp.clip(1.0 + 0.18 * jax.random.normal(keys[1], (D,), jnp.float32), 0.1, 1.9)
    expert_ids_keys = jax.random.split(jax.random.fold_in(keys[2], 1), TOKENS // TOK_GROUP)
    expert_ids_turns = jax.random.permutation(jax.random.fold_in(keys[2], 3), TOKENS // TOK_GROUP)
    expert_ids = jax.vmap(lambda own, number: shared_out(jax.random.fold_in(keys[2], 2), own, number, TOK_GROUP, EXPERTS, 2, CAP, 2))(expert_ids_keys, expert_ids_turns).reshape((TOKENS, 2))
    gate_weights = jnp.clip(0.1 + 0.79999997 * jax.random.uniform(keys[3], (TOKENS, 2), jnp.float32) ** shard_levels(keys[3], (TOKENS, 2), ((0, 4),), -0.2, 0.2), 0.1, 0.9)
    w_gate = bell_draw(keys[4], (EXPERTS, D, FF), D ** -0.5, 0.078125, ((0, 4), (2, 8)))
    w_up = bell_draw(keys[5], (EXPERTS, D, FF), D ** -0.5, 0.078125, ((0, 4), (2, 8)))
    w_down = bell_draw(keys[6], (EXPERTS, FF, D), FF ** -0.5, 0.0546875, ((0, 4), (1, 4), (2, 2)))
    label_rows = draw_label_rows(jax.random.fold_in(keys[11], 71), 0)
    seg_ids = jax.vmap(lambda own: jnp.searchsorted(jnp.cumsum(ragged_sizes(own, SEQS, TOK_GROUP, SEQ_MOST, 1)), jnp.arange(TOK_GROUP), side="right"))(jax.random.split(keys[8], DPG)).reshape((DPG, TOK_GROUP)).astype(jnp.int32)
    pair_slot = jax.vmap(lambda own: jax.random.permutation(own, SEQS))(jax.random.split(keys[9], DPG)).reshape((DPG, SEQS)).astype(jnp.int32)
    ref_scores = bell_draw(keys[10], (DPG, SEQS), 2.0, 8.0, ((0, 4),), jnp.float32)
    return {"tokens": tokens, "norm_gain": norm_gain, "expert_ids": expert_ids, "gate_weights": gate_weights, "w_gate": w_gate, "w_up": w_up, "w_down": w_down, "label_rows": label_rows, "seg_ids": seg_ids, "pair_slot": pair_slot, "ref_scores": ref_scores}


epsilon = 1e-05
dpo_beta = 0.5

def normed_rows(tokens, norm_gain):
    values = tokens.astype(jnp.float32)
    inverse_rms = lax.rsqrt(lax.optimization_barrier(jnp.mean(values * values, axis=1, keepdims=True)) + epsilon)
    return (values * inverse_rms * norm_gain[None, :].astype(jnp.float32)).astype(jnp.bfloat16)

def slot_tables(expert_ids, gate_weights, experts, capacity):
    tok_count = expert_ids.shape[0]
    flat_ids = expert_ids.reshape(-1).astype(jnp.int32)
    onehot = (flat_ids[:, None] == jnp.arange(experts, dtype=jnp.int32)[None, :]).astype(jnp.int32)
    earlier = jnp.cumsum(onehot, axis=0).astype(jnp.int32) - onehot
    position = lax.optimization_barrier(jnp.sum(earlier * onehot, axis=1)).astype(jnp.int32)
    slot_index = flat_ids * capacity + position
    slot_match = (slot_index[:, None] == jnp.arange(experts * capacity, dtype=jnp.int32)[None, :]).astype(jnp.float32)
    slot_match = slot_match.reshape(tok_count, 2, experts * capacity)
    placement = lax.optimization_barrier(jnp.sum(slot_match, axis=1))
    mixing = lax.optimization_barrier(jnp.sum(slot_match * gate_weights[:, :, None].astype(jnp.float32), axis=1))
    return (placement, mixing)

def rounded_term(value):
    narrow = lax.optimization_barrier(value.astype(jnp.bfloat16))
    return narrow.astype(jnp.float32)

def run_expert(operands):
    rows, gate_matrix, up_matrix, down_matrix = operands
    gate_sum = jnp.dot(rows, gate_matrix, preferred_element_type=jnp.float32)
    up_sum = jnp.dot(rows, up_matrix, preferred_element_type=jnp.float32)
    hidden = (jax.nn.silu(gate_sum) * up_sum).astype(jnp.bfloat16)
    block = FF // N_DP
    total = jnp.zeros((rows.shape[0], down_matrix.shape[1]), jnp.float32)
    for index in range(N_DP):
        piece = jnp.dot(hidden[:, index * block:(index + 1) * block], down_matrix[index * block:(index + 1) * block], preferred_element_type=jnp.float32)
        total = total + rounded_term(piece)
    return total.astype(jnp.bfloat16)

def reference(tokens, norm_gain, expert_ids, gate_weights, w_gate, w_up, w_down, label_rows, seg_ids, pair_slot, ref_scores):
    groups = N_DP
    normed = normed_rows(tokens, norm_gain).reshape(groups, TOK_GROUP, D)
    tables = partial(slot_tables, experts=EXPERTS, capacity=CAP)
    placement, mixing = jax.vmap(tables)(expert_ids.reshape(groups, TOK_GROUP, 2), gate_weights.reshape(groups, TOK_GROUP, 2))
    outgoing = jnp.einsum('gts,gtd->gsd', placement.astype(jnp.float32), normed.astype(jnp.float32)).astype(jnp.bfloat16)
    by_expert = outgoing.reshape(groups, EXPERTS, CAP, D).transpose(1, 0, 2, 3).reshape(EXPERTS, groups * CAP, D)
    expert_out = lax.map(run_expert, (by_expert, w_gate, w_up, w_down))
    per_expert = expert_out.reshape(EXPERTS, groups, CAP, D)
    mixing_parts = mixing.reshape(groups, TOK_GROUP, EXPERTS, CAP)
    expert_mix = jnp.zeros((groups, TOK_GROUP, D), jnp.float32)
    for expert in range(EXPERTS):
        term = jnp.einsum('gtc,gcd->gtd', mixing_parts[:, :, expert, :], per_expert[expert].astype(jnp.float32), precision=lax.Precision.HIGHEST)
        expert_mix = expert_mix + rounded_term(term)
    mixed = tokens.astype(jnp.float32) + expert_mix.reshape(TOKENS, D)
    layer_out = mixed.astype(jnp.bfloat16)
    token_score = lax.optimization_barrier(jnp.sum(mixed * label_rows.astype(jnp.float32), axis=1)).reshape(N_DP, TOK_GROUP)
    member = (seg_ids[:, :, None] == jnp.arange(SEQS, dtype=jnp.int32)[None, None, :]).astype(jnp.float32)
    totals = lax.optimization_barrier(jnp.sum(member * token_score[:, :, None], axis=1))
    polarity = (1 - 2 * (pair_slot % 2)).astype(jnp.float32)
    pair_member = ((pair_slot // 2)[:, :, None] == jnp.arange(PAIRS, dtype=jnp.int32)[None, None, :]).astype(jnp.float32)
    margins = dpo_beta * lax.optimization_barrier(jnp.sum(pair_member * (polarity * (totals - ref_scores))[:, :, None], axis=1))
    return (layer_out, margins)
```

```python
import functools

import jax
import jax.numpy as jnp
from jax import lax
from jax.experimental import pallas as pl
from jax.experimental.pallas import tpu as pltpu
from jax.sharding import PartitionSpec as P

SEQS = 4
PAIRS = 2
LANES = 128
epsilon = 1e-05
dpo_beta = 0.5
F32 = jnp.float32
BF16 = jnp.bfloat16
MESH = pl.DeviceIdType.MESH


def dims(mesh_shape, group, width, hidden):
    dp, ex, tn = mesh_shape
    cap = max(2, 9 * group // (4 * ex))
    cap_pad = -(-cap // 16) * 16
    piece = width // (ex * tn)
    chunks = 3 if piece % 384 == 0 else 1
    sub = piece // chunks
    h_tile = 256 if hidden % 256 == 0 else 128
    p_tile = 256 if piece % 256 == 0 else 128
    return dp, ex, tn, cap_pad, piece, chunks, sub, h_tile, p_tile


def kernel(
    size, tokens, gain, meta_in, label, member, w_gate, w_up, w_down,
    out, totals,
    normed, meta, tok, pack, rows, wg, wu, wd, acc_g, acc_u, hid, dn_out, dn_in,
    mix_out, mix_in, tr_out, tr_in, sc_out, sc_in,
    w_sem, d_sem, meta_s, meta_r, z_s, z_r, x_s, x_r, f_s, f_r, h_s, h_r,
    n_s, n_r, m_s, m_r, t_s, t_r, c_s, c_r,
):
    dp, ex, tn, cap, piece, chunks, sub, h_tile, p_tile = size
    group, width = tokens.shape
    half = width // tn
    hidden = w_gate.shape[2]
    depth = ex * tn * sub
    count = group // ex
    g, e, t = lax.axis_index("dp"), lax.axis_index("expert"), lax.axis_index("tensor")
    slots = min(chunks, 2)
    d_slots = wd.shape[0]
    sent = []

    def at_dp(k):
        return (lax.rem(g + k, dp), e, t)

    def at_ex(k):
        return (g, lax.rem(e + k, ex), t)

    def at_tn(k):
        return (g, e, lax.rem(t + k, tn))

    def remote(src, dst, s, r, dev):
        return pltpu.make_async_remote_copy(
            src_ref=src, dst_ref=dst, send_sem=s, recv_sem=r, device_id=dev, device_id_type=MESH
        )

    def send(*a):
        c = remote(*a)
        c.start()
        sent.append(c)

    def load_chunk(s):
        for i, (src, dst) in enumerate(((w_gate, wg), (w_up, wu))):
            for q in range(ex * tn):
                pltpu.make_async_copy(
                    src.at[0, pl.ds(q * piece + s * sub, sub)],
                    dst.at[s % slots, pl.ds(q * sub, sub)],
                    w_sem.at[i, s],
                ).start()

    def wait_chunk(s):
        for i, (src, dst) in enumerate(((w_gate, wg), (w_up, wu))):
            pltpu.make_async_copy(src.at[0, pl.ds(0, depth)], dst.at[s % slots], w_sem.at[i, s]).wait()

    def down_copy(i):
        owner = lax.rem(e + i + 1, ex)
        return pltpu.make_async_copy(
            w_down.at[0, :, pl.ds(pl.multiple_of(owner * piece, LANES), piece)],
            wd.at[i % d_slots],
            d_sem.at[i],
        )

    for s in range(slots):
        load_chunk(s)
    for i in range(d_slots):
        down_copy(i).start()

    barrier = pltpu.get_barrier_semaphore()
    peers = 0
    for k in range(1, dp):
        pl.semaphore_signal(barrier, inc=1, device_id=at_dp(k), device_id_type=MESH)
        peers += 1
    for k in range(ex):
        for j in range(tn):
            if k or j:
                dev = (g, lax.rem(e + k, ex), lax.rem(t + j, tn))
                pl.semaphore_signal(barrier, inc=1, device_id=dev, device_id_type=MESH)
                peers += 1

    step = 16

    @pl.loop(0, group // step)
    def _(i):
        at = pl.ds(pl.multiple_of(i * step, step), step)
        v = tokens[at, :].astype(F32)
        inv = lax.rsqrt(jnp.mean(v * v, axis=1, keepdims=True) + epsilon)
        normed[at, :] = (v * inv * gain[...]).astype(BF16)

    info = meta_in[...]
    eid = lax.broadcasted_iota(jnp.int32, (16, group), 0).astype(F32)
    id0, id1 = info[2:3, :], info[3:4, :]
    hit0, hit1 = eid == id0, eid == id1
    named = jnp.where(hit0 | hit1, 1.0, 0.0).astype(BF16)
    tri = (
        lax.broadcasted_iota(jnp.int32, (group, group), 0)
        < lax.broadcasted_iota(jnp.int32, (group, group), 1)
    )
    earlier = jnp.dot(named, jnp.where(tri, 1.0, 0.0).astype(BF16), preferred_element_type=F32)
    pos0 = jnp.sum(jnp.where(hit0, earlier, 0.0), axis=0, keepdims=True)
    pos1 = jnp.sum(jnp.where(hit1, earlier, 0.0), axis=0, keepdims=True)
    s0, s1 = id0 * cap + pos0, id1 * cap + pos1
    r8 = lax.broadcasted_iota(jnp.int32, (8, group), 0)
    meta[0] = jnp.where(r8 == 2, s0, jnp.where(r8 == 3, s1, info))

    pl.semaphore_wait(barrier, peers)

    my_col = pl.multiple_of(t * half + e * piece, LANES)
    for k in range(1, dp):
        send(meta.at[0], meta.at[dp - k], meta_s.at[k], meta_r.at[dp - k], at_dp(k))
    for s in range(chunks):
        for k in range(1, dp):
            send(
                normed.at[:, pl.ds(pl.multiple_of(my_col + s * sub, LANES), sub)],
                tok.at[s, dp - k],
                z_s.at[s, k], z_r.at[s, dp - k], at_dp(k),
            )

    row_id = lax.broadcasted_iota(jnp.int32, (cap, group), 0).astype(F32) + (e * cap).astype(F32)
    own_hot = jnp.where((row_id == s0) | (row_id == s1), 1.0, 0.0).astype(BF16)
    for s in range(chunks):
        for q in range(ex * tn):
            rows[s, 0, :, q * sub:(q + 1) * sub] = jnp.dot(
                own_hot, normed[:, q * piece + s * sub:q * piece + (s + 1) * sub],
                preferred_element_type=F32,
            ).astype(BF16)

    all_id = lax.broadcasted_iota(jnp.int32, (ex * cap, group), 0).astype(F32)
    mine = t * ex + e

    def block(q):
        return pl.ds(pl.multiple_of(q * sub, LANES), sub)

    def forward(s, owner, k):
        for j in range(1, tn):
            ref = rows.at[s, pl.ds(1, dp - 1), :, block(t * ex + owner)]
            send(ref, ref, f_s.at[s, k, j], f_r.at[s, k, tn - j], at_tn(j))

    def pack_chunk(s):
        for d in range(1, dp):
            if s == 0:
                remote(meta.at[0], meta.at[d], meta_s.at[d], meta_r.at[d], at_dp(d)).wait_recv()
            remote(tok.at[s, d], tok.at[s, d], z_s.at[s, d], z_r.at[s, d], at_dp(d)).wait_recv()
            hot = jnp.where((all_id == meta[d, 2:3, :]) | (all_id == meta[d, 3:4, :]), 1.0, 0.0)
            got = jnp.dot(hot.astype(BF16), tok[s, d], preferred_element_type=F32)
            got = got.astype(BF16).reshape(ex, cap, sub)
            for x in range(ex):
                pack[s, x, d - 1] = got[x]
            rows[s, d, :, block(mine)] = pack[s, e, d - 1]
        for k in range(1, ex):
            send(
                pack.at[s, lax.rem(e + k, ex)],
                rows.at[s, pl.ds(1, dp - 1), :, block(mine)],
                x_s.at[s, k], x_r.at[s, ex - k], at_ex(k),
            )
        forward(s, e, 0)

    def forward_chunk(s):
        for k in range(1, ex):
            owner = lax.rem(e + k, ex)
            ref = rows.at[s, pl.ds(1, dp - 1), :, block(t * ex + owner)]
            remote(ref, ref, x_s.at[s, k], x_r.at[s, k], at_ex(k)).wait_recv()
            forward(s, owner, k)

    def sibling_wait(s):
        for j in range(1, tn):
            for k in range(ex):
                other = lax.rem(t + j, tn) * ex + lax.rem(e + k, ex)
                ref = rows.at[s, pl.ds(1, dp - 1), :, block(other)]
                remote(ref, ref, f_s.at[s, k, j], f_r.at[s, k, j], at_tn(j)).wait_recv()

    n_h = hidden // h_tile

    def hid_copy(n, j):
        ref = hid.at[t, :, pl.ds(pl.multiple_of(n * h_tile, LANES), h_tile)]
        return remote(ref, ref, h_s.at[j, n], h_r.at[tn - j, n], at_tn(j))

    def compute(s):
        wait_chunk(s)
        last = s == chunks - 1

        @pl.loop(0, n_h)
        def _(n):
            at = pl.ds(pl.multiple_of(n * h_tile, LANES), h_tile)
            x = rows[s].reshape(dp * cap, depth)
            a = jnp.dot(x, wg[s % slots, :, at], preferred_element_type=F32)
            b = jnp.dot(x, wu[s % slots, :, at], preferred_element_type=F32)
            if s > 0:
                a = a + acc_g[:, at]
                b = b + acc_u[:, at]
            if last:
                hid[t, :, at] = (a / (1.0 + jnp.exp(-a)) * b).astype(BF16)
                for j in range(1, tn):
                    hid_copy(n, j).start()
            else:
                acc_g[:, at] = a
                acc_u[:, at] = b

    pack_chunk(0)
    for s in range(chunks):
        forward_chunk(s)
        if s + 1 < chunks:
            pack_chunk(s + 1)
        sibling_wait(s)
        compute(s)
        if s + slots < chunks:
            load_chunk(s + slots)

    for j in range(1, tn):
        other = lax.rem(t + j, tn)

        @pl.loop(0, n_h)
        def _(n):
            ref = hid.at[other, :, pl.ds(pl.multiple_of(n * h_tile, LANES), h_tile)]
            remote(ref, ref, h_s.at[j, n], h_r.at[j, n], at_tn(j)).wait_recv()

    for i in range(ex):
        k = (i + 1) % ex
        down_copy(i).wait()

        @pl.loop(0, piece // p_tile)
        def _(n):
            at = pl.ds(pl.multiple_of(n * p_tile, LANES), p_tile)
            y = jnp.zeros((dp * cap, p_tile), F32)
            for j in range(tn):
                y = y + jnp.dot(
                    hid[j], wd[i % d_slots, j * hidden:(j + 1) * hidden, at], preferred_element_type=F32
                )
            y = y.astype(BF16).reshape(dp, cap, p_tile)
            if k:
                dn_out[k - 1, :, :, at] = y
            else:
                dn_in[:, e, :, at] = y

        if k:
            send(dn_out.at[k - 1], dn_in.at[:, e], n_s.at[k], n_r.at[ex - k], at_ex(k))
        if i + d_slots < ex:
            down_copy(i + d_slots).start()
    for k in range(1, ex):
        ref = dn_in.at[:, lax.rem(e + k, ex)]
        remote(ref, ref, n_s.at[k], n_r.at[k], at_ex(k)).wait_recv()

    slot_id = lax.broadcasted_iota(jnp.int32, (group, ex * cap), 1).astype(F32)
    own_mix = None
    for i in range(dp):
        d = (i + 1) % dp
        m = jnp.transpose(meta[d])
        w = jnp.where(slot_id == m[:, 2:3], m[:, 0:1], 0.0)
        w = w + jnp.where(slot_id == m[:, 3:4], m[:, 1:2], 0.0)
        y = jnp.dot(
            w.astype(BF16), dn_in[d].reshape(ex * cap, piece), preferred_element_type=F32
        ).astype(BF16)
        if d:
            mix_out[d - 1] = y
            send(mix_out.at[d - 1], mix_in.at[dp - d], m_s.at[d], m_r.at[dp - d], at_dp(d))
        else:
            mix_in[0] = y
    for d in range(1, dp):
        remote(mix_in.at[d], mix_in.at[d], m_s.at[d], m_r.at[d], at_dp(d)).wait_recv()
    for x in range(ex):
        total = jnp.zeros((count, piece), F32)
        for d in range(dp):
            total = total + mix_in[d, x * count:(x + 1) * count, :].astype(F32)
        tr_out[x] = total.astype(BF16)
    for k in range(1, ex):
        send(tr_out.at[lax.rem(e + k, ex)], tr_in.at[e], t_s.at[k], t_r.at[ex - k], at_ex(k))
    tr_in[e] = tr_out[e]
    for k in range(1, ex):
        ref = tr_in.at[lax.rem(e + k, ex)]
        remote(ref, ref, t_s.at[k], t_r.at[k], at_ex(k)).wait_recv()

    score = jnp.zeros((count, 1), F32)
    own_rows = pl.ds(pl.multiple_of(e * count, 16), count)
    for x in range(ex):
        cols = pl.ds(pl.multiple_of(t * half + x * piece, LANES), piece)
        mixed = tokens[own_rows, cols].astype(F32) + tr_in[x].astype(F32)
        out[:, x * piece:(x + 1) * piece] = mixed.astype(BF16)
        lab = label[:, x * piece:(x + 1) * piece].astype(F32)
        score = score + jnp.sum(mixed * lab, axis=1, keepdims=True)
    part = jnp.sum(member[own_rows, :] * score, axis=0, keepdims=True)
    sc_out[...] = jnp.broadcast_to(part, (8, LANES))
    pairs = [(k, j) for k in range(ex) for j in range(tn) if k or j]
    for k, j in pairs:
        back = ((ex - k) % ex) * tn + (tn - j) % tn
        dev = (g, lax.rem(e + k, ex), lax.rem(t + j, tn))
        send(sc_out, sc_in.at[back], c_s.at[k * tn + j], c_r.at[back], dev)
    seq = sc_out[...]
    for k, j in pairs:
        n = k * tn + j
        dev = (g, lax.rem(e + k, ex), lax.rem(t + j, tn))
        remote(sc_out, sc_in.at[n], c_s.at[n], c_r.at[n], dev).wait_recv()
        seq = seq + sc_in[n]
    totals[...] = seq

    for c in sent:
        c.wait_send()
    for j in range(1, tn):

        @pl.loop(0, n_h)
        def _(n):
            hid_copy(n, j).wait_send()


def body(
    mesh_shape, tokens, norm_gain, expert_ids, gate_weights, w_gate, w_up, w_down,
    label_rows, seg_ids, pair_slot, ref_scores,
):
    group, width = tokens.shape
    hidden = w_gate.shape[2]
    size = dims(mesh_shape, group, width, hidden)
    dp, ex, tn, cap, piece, chunks, sub, h_tile, p_tile = size
    depth = ex * tn * sub
    slots = min(chunks, 2)
    d_slots = min(ex, 2)
    count = group // ex
    half = width // tn
    n_h = hidden // h_tile
    meta = jnp.concatenate(
        [gate_weights.T, expert_ids.T.astype(F32), jnp.zeros((4, group), F32)], axis=0
    )
    member = (seg_ids[0][:, None] == jnp.arange(LANES, dtype=jnp.int32)[None, :]).astype(F32)
    vm = pl.BlockSpec(memory_space=pltpu.VMEM)
    hbm = pl.BlockSpec(memory_space=pl.ANY)
    dma = pltpu.SemaphoreType.DMA
    scratch = [
        pltpu.VMEM((group, width), BF16),
        pltpu.VMEM((dp, 8, group), F32),
        pltpu.VMEM((chunks, dp, group, sub), BF16),
        pltpu.VMEM((chunks, ex, dp - 1, cap, sub), BF16),
        pltpu.VMEM((chunks, dp, cap, depth), BF16),
        pltpu.VMEM((slots, depth, hidden), BF16),
        pltpu.VMEM((slots, depth, hidden), BF16),
        pltpu.VMEM((d_slots, w_down.shape[1], piece), BF16),
        pltpu.VMEM((dp * cap, hidden), F32),
        pltpu.VMEM((dp * cap, hidden), F32),
        pltpu.VMEM((tn, dp * cap, hidden), BF16),
        pltpu.VMEM((ex - 1, dp, cap, piece), BF16),
        pltpu.VMEM((dp, ex, cap, piece), BF16),
        pltpu.VMEM((dp - 1, group, piece), BF16),
        pltpu.VMEM((dp, group, piece), BF16),
        pltpu.VMEM((ex, count, piece), BF16),
        pltpu.VMEM((ex, count, piece), BF16),
        pltpu.VMEM((8, LANES), F32),
        pltpu.VMEM((ex * tn, 8, LANES), F32),
        dma((2, chunks)), dma((ex,)),
        dma((dp,)), dma((dp,)),
        dma((chunks, dp)), dma((chunks, dp)),
        dma((chunks, ex)), dma((chunks, ex)),
        dma((chunks, ex, tn)), dma((chunks, ex, tn)),
        dma((tn, n_h)), dma((tn, n_h)),
        dma((ex,)), dma((ex,)),
        dma((dp,)), dma((dp,)),
        dma((ex,)), dma((ex,)),
        dma((ex * tn,)), dma((ex * tn,)),
    ]
    layer_out, totals = pl.pallas_call(
        functools.partial(kernel, size),
        out_shape=(
            jax.ShapeDtypeStruct((count, half), BF16),
            jax.ShapeDtypeStruct((8, LANES), F32),
        ),
        in_specs=[vm, vm, vm, vm, vm, hbm, hbm, hbm],
        out_specs=(vm, vm),
        scratch_shapes=scratch,
        compiler_params=pltpu.CompilerParams(
            collective_id=0, has_side_effects=True, vmem_limit_bytes=66_000_000
        ),
    )(tokens, norm_gain[None, :], meta, label_rows, member, w_gate, w_up, w_down)
    seq_totals = totals[0, :SEQS]
    slots_here = pair_slot[0]
    polarity = (1 - 2 * (slots_here % 2)).astype(F32)
    pair_member = (
        (slots_here // 2)[:, None] == jnp.arange(PAIRS, dtype=jnp.int32)[None, :]
    ).astype(F32)
    margins = dpo_beta * jnp.sum(
        pair_member * (polarity * (seq_totals - ref_scores[0]))[:, None], axis=0
    )
    return (layer_out, margins[None, :])


def solution(mesh):
    placed = (
        P("dp", None),
        P(),
        P("dp", None),
        P("dp", None),
        P("expert", None, ("dp", "tensor")),
        P("expert", None, ("dp", "tensor")),
        P("expert", "dp", "tensor"),
        P(("dp", "expert"), "tensor"),
        P("dp", None),
        P("dp", None),
        P("dp", None),
    )
    mesh_shape = tuple(mesh.shape[name] for name in ("dp", "expert", "tensor"))
    return jax.shard_map(
        functools.partial(body, mesh_shape),
        mesh=mesh,
        in_specs=placed,
        out_specs=(P(("dp", "expert"), "tensor"), P("dp", None)),
        check_vma=False,
    )
```

```python
import functools

import jax
import jax.numpy as jnp
from jax import lax
from jax.experimental import pallas as pl
from jax.experimental.pallas import tpu as pltpu
from jax.sharding import PartitionSpec as P

SEQS = 4
PAIRS = 2
LANES = 128
epsilon = 1e-05
dpo_beta = 0.5
F32 = jnp.float32
BF16 = jnp.bfloat16
MESH = pl.DeviceIdType.MESH


def dims(mesh_shape, group, width, hidden):
    dp, ex, tn = mesh_shape
    cap = max(2, 9 * group // (4 * ex))
    cap_pad = -(-cap // 16) * 16
    piece = width // (ex * tn)
    chunks = 3 if piece % 384 == 0 else 1
    sub = piece // chunks
    h_tile = 256 if hidden % 256 == 0 else 128
    return dp, ex, tn, cap_pad, piece, chunks, sub, h_tile


def kernel(
    size, tokens, gain, meta_in, label, w_gate, w_up, w_down,
    out, totals,
    normed, meta, tok, pack, rows, wg, wu, wd, acc_g, acc_u, hid, dn_out, dn_in,
    mix_out, mix_in, mixing, member, tr_out, tr_in, sc_out, sc_in,
    w_sem, d_sem, meta_s, meta_r, z_s, z_r, x_s, x_r, f_s, f_r, h_s, h_r,
    n_s, n_r, m_s, m_r, t_s, t_r, c_s, c_r,
):
    dp, ex, tn, cap, piece, chunks, sub, h_tile = size
    group, width = tokens.shape
    half = width // tn
    hidden = w_gate.shape[2]
    depth = ex * tn * sub
    count = group // ex
    g, e, t = lax.axis_index("dp"), lax.axis_index("expert"), lax.axis_index("tensor")
    slots = min(chunks, 2)
    window = 1
    d_slots = wd.shape[0]
    n_down = chunks * ex
    sent = []

    def at_dp(k):
        return (lax.rem(g + k, dp), e, t)

    def at_ex(k):
        return (g, lax.rem(e + k, ex), t)

    def at_tn(k):
        return (g, e, lax.rem(t + k, tn))

    def remote(src, dst, s, r, dev):
        return pltpu.make_async_remote_copy(
            src_ref=src, dst_ref=dst, send_sem=s, recv_sem=r, device_id=dev, device_id_type=MESH
        )

    def send(*a):
        c = remote(*a)
        c.start()
        sent.append(c)

    def load_chunk(s):
        for i, (src, dst) in enumerate(((w_gate, wg), (w_up, wu))):
            for q in range(ex * tn):
                pltpu.make_async_copy(
                    src.at[0, pl.ds(q * piece + s * sub, sub)],
                    dst.at[s % slots, pl.ds(q * sub, sub)],
                    w_sem.at[i, s],
                ).start()

    def wait_chunk(s):
        for i, (src, dst) in enumerate(((w_gate, wg), (w_up, wu))):
            pltpu.make_async_copy(src.at[0, pl.ds(0, depth)], dst.at[s % slots], w_sem.at[i, s]).wait()

    def down_copy(i):
        start = lax.rem(e + i + 1, ex) * piece + (i // ex) * sub
        return pltpu.make_async_copy(
            w_down.at[0, :, pl.ds(pl.multiple_of(start, LANES), sub)],
            wd.at[i % d_slots],
            d_sem.at[i],
        )

    for s in range(slots):
        load_chunk(s)
    for i in range(d_slots):
        down_copy(i).start()

    barrier = pltpu.get_barrier_semaphore()
    peers = 0
    for k in range(1, dp):
        pl.semaphore_signal(barrier, inc=1, device_id=at_dp(k), device_id_type=MESH)
        peers += 1
    for k in range(ex):
        for j in range(tn):
            if k or j:
                dev = (g, lax.rem(e + k, ex), lax.rem(t + j, tn))
                pl.semaphore_signal(barrier, inc=1, device_id=dev, device_id_type=MESH)
                peers += 1

    step = 16

    @pl.loop(0, group // step)
    def _(i):
        at = pl.ds(pl.multiple_of(i * step, step), step)
        v = tokens[at, :].astype(F32)
        inv = lax.rsqrt(jnp.mean(v * v, axis=1, keepdims=True) + epsilon)
        normed[at, :] = (v * inv * gain[...]).astype(BF16)

    info = meta_in[...]
    eid = lax.broadcasted_iota(jnp.int32, (16, group), 0).astype(F32)
    id0, id1 = info[2:3, :], info[3:4, :]
    hit0, hit1 = eid == id0, eid == id1
    named = jnp.where(hit0 | hit1, 1.0, 0.0).astype(BF16)
    tri = (
        lax.broadcasted_iota(jnp.int32, (group, group), 0)
        < lax.broadcasted_iota(jnp.int32, (group, group), 1)
    )
    earlier = jnp.dot(named, jnp.where(tri, 1.0, 0.0).astype(BF16), preferred_element_type=F32)
    pos0 = jnp.sum(jnp.where(hit0, earlier, 0.0), axis=0, keepdims=True)
    pos1 = jnp.sum(jnp.where(hit1, earlier, 0.0), axis=0, keepdims=True)
    s0, s1 = id0 * cap + pos0, id1 * cap + pos1
    r8 = lax.broadcasted_iota(jnp.int32, (8, group), 0)
    meta[0] = jnp.where(r8 == 2, s0, jnp.where(r8 == 3, s1, info))

    pl.semaphore_wait(barrier, peers)

    my_col = pl.multiple_of(t * half + e * piece, LANES)
    for k in range(1, dp):
        send(meta.at[0], meta.at[dp - k], meta_s.at[k], meta_r.at[dp - k], at_dp(k))

    def send_tokens(s):
        for k in range(1, dp):
            send(
                normed.at[:, pl.ds(pl.multiple_of(my_col + s * sub, LANES), sub)],
                tok.at[s, dp - k],
                z_s.at[s, k], z_r.at[s, dp - k], at_dp(k),
            )

    for s in range(min(chunks, window)):
        send_tokens(s)

    row_id = lax.broadcasted_iota(jnp.int32, (cap, group), 0).astype(F32) + (e * cap).astype(F32)
    own_hot = jnp.where((row_id == s0) | (row_id == s1), 1.0, 0.0).astype(BF16)
    for s in range(chunks):
        for q in range(ex * tn):
            rows[s, 0, :, q * sub:(q + 1) * sub] = jnp.dot(
                own_hot, normed[:, q * piece + s * sub:q * piece + (s + 1) * sub],
                preferred_element_type=F32,
            ).astype(BF16)

    all_id = lax.broadcasted_iota(jnp.int32, (ex * cap, group), 0).astype(F32)
    mine = t * ex + e

    def block(q):
        return pl.ds(pl.multiple_of(q * sub, LANES), sub)

    def forward(s, owner, k):
        for j in range(1, tn):
            ref = rows.at[s, pl.ds(1, dp - 1), :, block(t * ex + owner)]
            send(ref, ref, f_s.at[s, k, j], f_r.at[s, k, tn - j], at_tn(j))

    def pack_chunk(s):
        for d in range(1, dp):
            if s == 0:
                remote(meta.at[0], meta.at[d], meta_s.at[d], meta_r.at[d], at_dp(d)).wait_recv()
            remote(tok.at[s, d], tok.at[s, d], z_s.at[s, d], z_r.at[s, d], at_dp(d)).wait_recv()
            hot = jnp.where((all_id == meta[d, 2:3, :]) | (all_id == meta[d, 3:4, :]), 1.0, 0.0)
            got = jnp.dot(hot.astype(BF16), tok[s, d], preferred_element_type=F32)
            got = got.astype(BF16).reshape(ex, cap, sub)
            for x in range(ex):
                pack[s, x, d - 1] = got[x]
            rows[s, d, :, block(mine)] = pack[s, e, d - 1]
        if s + window < chunks:
            send_tokens(s + window)
        for k in range(1, ex):
            send(
                pack.at[s, lax.rem(e + k, ex)],
                rows.at[s, pl.ds(1, dp - 1), :, block(mine)],
                x_s.at[s, k], x_r.at[s, ex - k], at_ex(k),
            )
        forward(s, e, 0)

    def forward_chunk(s):
        for k in range(1, ex):
            owner = lax.rem(e + k, ex)
            ref = rows.at[s, pl.ds(1, dp - 1), :, block(t * ex + owner)]
            remote(ref, ref, x_s.at[s, k], x_r.at[s, k], at_ex(k)).wait_recv()
            forward(s, owner, k)

    def sibling_wait(s):
        for j in range(1, tn):
            for k in range(ex):
                other = lax.rem(t + j, tn) * ex + lax.rem(e + k, ex)
                ref = rows.at[s, pl.ds(1, dp - 1), :, block(other)]
                remote(ref, ref, f_s.at[s, k, j], f_r.at[s, k, j], at_tn(j)).wait_recv()

    n_h = hidden // h_tile

    def hid_copy(n, j):
        ref = hid.at[t, :, pl.ds(pl.multiple_of(n * h_tile, LANES), h_tile)]
        return remote(ref, ref, h_s.at[j, n], h_r.at[tn - j, n], at_tn(j))

    def compute(s):
        wait_chunk(s)
        last = s == chunks - 1

        @pl.loop(0, n_h)
        def _(n):
            at = pl.ds(pl.multiple_of(n * h_tile, LANES), h_tile)
            x = rows[s].reshape(dp * cap, depth)
            a = jnp.dot(x, wg[s % slots, :, at], preferred_element_type=F32)
            b = jnp.dot(x, wu[s % slots, :, at], preferred_element_type=F32)
            if s > 0:
                a = a + acc_g[:, at]
                b = b + acc_u[:, at]
            if last:
                hid[t, :, at] = (a / (1.0 + jnp.exp(-a)) * b).astype(BF16)
                for j in range(1, tn):
                    hid_copy(n, j).start()
            else:
                acc_g[:, at] = a
                acc_u[:, at] = b

    pack_chunk(0)
    for s in range(chunks):
        forward_chunk(s)
        if s + 1 < chunks:
            pack_chunk(s + 1)
        sibling_wait(s)
        compute(s)
        if s + slots < chunks:
            load_chunk(s + slots)

    for j in range(1, tn):
        other = lax.rem(t + j, tn)

        @pl.loop(0, n_h)
        def _(n):
            ref = hid.at[other, :, pl.ds(pl.multiple_of(n * h_tile, LANES), h_tile)]
            remote(ref, ref, h_s.at[j, n], h_r.at[j, n], at_tn(j)).wait_recv()

    for i in range(n_down):
        c, k = i // ex, (i + 1) % ex
        down_copy(i).wait()
        y = jnp.zeros((dp * cap, sub), F32)
        for j in range(tn):
            y = y + jnp.dot(
                hid[j], wd[i % d_slots, j * hidden:(j + 1) * hidden, :], preferred_element_type=F32
            )
        y = y.astype(BF16).reshape(dp, cap, sub)
        if k:
            dn_out[c, k - 1] = y
            send(dn_out.at[c, k - 1], dn_in.at[c, :, e], n_s.at[c, k], n_r.at[c, ex - k], at_ex(k))
        else:
            dn_in[c, :, e] = y
        if i + d_slots < n_down:
            down_copy(i + d_slots).start()

    slot_id = lax.broadcasted_iota(jnp.int32, (group, ex * cap), 1).astype(F32)
    for d in range(dp):
        m = jnp.transpose(meta[d])
        w = jnp.where(slot_id == m[:, 2:3], m[:, 0:1], 0.0)
        w = w + jnp.where(slot_id == m[:, 3:4], m[:, 1:2], 0.0)
        mixing[d] = w.astype(BF16)
        if d == 0:
            seq_id = lax.broadcasted_iota(jnp.int32, (group, LANES), 1).astype(F32)
            member[...] = jnp.where(seq_id == m[:, 4:5], 1.0, 0.0)
    for c in range(chunks):
        for k in range(1, ex):
            ref = dn_in.at[c, :, lax.rem(e + k, ex)]
            remote(ref, ref, n_s.at[c, k], n_r.at[c, k], at_ex(k)).wait_recv()
        for i in range(dp):
            d = (i + 1) % dp
            y = jnp.dot(
                mixing[d], dn_in[c, d].reshape(ex * cap, sub), preferred_element_type=F32
            ).astype(BF16)
            if d:
                mix_out[c, d - 1] = y
                send(
                    mix_out.at[c, d - 1], mix_in.at[c, dp - d],
                    m_s.at[c, d], m_r.at[c, dp - d], at_dp(d),
                )
            else:
                mix_in[c, 0] = y
    for c in range(chunks):
        for d in range(1, dp):
            ref = mix_in.at[c, d]
            remote(ref, ref, m_s.at[c, d], m_r.at[c, d], at_dp(d)).wait_recv()
        for x in range(ex):
            total = jnp.zeros((count, sub), F32)
            for d in range(dp):
                total = total + mix_in[c, d, x * count:(x + 1) * count, :].astype(F32)
            tr_out[c, x] = total.astype(BF16)
        for k in range(1, ex):
            send(
                tr_out.at[c, lax.rem(e + k, ex)], tr_in.at[c, e],
                t_s.at[c, k], t_r.at[c, ex - k], at_ex(k),
            )
        tr_in[c, e] = tr_out[c, e]

    score = jnp.zeros((count, 1), F32)
    own_rows = pl.ds(pl.multiple_of(e * count, 16), count)
    for c in range(chunks):
        for k in range(1, ex):
            ref = tr_in.at[c, lax.rem(e + k, ex)]
            remote(ref, ref, t_s.at[c, k], t_r.at[c, k], at_ex(k)).wait_recv()
        for x in range(ex):
            low = x * piece + c * sub
            cols = pl.ds(pl.multiple_of(t * half + low, LANES), sub)
            mixed = tokens[own_rows, cols].astype(F32) + tr_in[c, x].astype(F32)
            out[:, low:low + sub] = mixed.astype(BF16)
            lab = label[:, low:low + sub].astype(F32)
            score = score + jnp.sum(mixed * lab, axis=1, keepdims=True)
    part = jnp.sum(member[own_rows, :] * score, axis=0, keepdims=True)
    sc_out[...] = jnp.broadcast_to(part, (8, LANES))
    pairs = [(k, j) for k in range(ex) for j in range(tn) if k or j]
    for k, j in pairs:
        back = ((ex - k) % ex) * tn + (tn - j) % tn
        dev = (g, lax.rem(e + k, ex), lax.rem(t + j, tn))
        send(sc_out, sc_in.at[back], c_s.at[k * tn + j], c_r.at[back], dev)
    seq = sc_out[...]
    for k, j in pairs:
        n = k * tn + j
        dev = (g, lax.rem(e + k, ex), lax.rem(t + j, tn))
        remote(sc_out, sc_in.at[n], c_s.at[n], c_r.at[n], dev).wait_recv()
        seq = seq + sc_in[n]
    totals[...] = seq

    for c in sent:
        c.wait_send()
    for j in range(1, tn):

        @pl.loop(0, n_h)
        def _(n):
            hid_copy(n, j).wait_send()


def body(
    mesh_shape, tokens, norm_gain, expert_ids, gate_weights, w_gate, w_up, w_down,
    label_rows, seg_ids, pair_slot, ref_scores,
):
    group, width = tokens.shape
    hidden = w_gate.shape[2]
    size = dims(mesh_shape, group, width, hidden)
    dp, ex, tn, cap, piece, chunks, sub, h_tile = size
    depth = ex * tn * sub
    slots = min(chunks, 2)
    d_slots = min(chunks * ex, 2 * chunks)
    count = group // ex
    half = width // tn
    n_h = hidden // h_tile
    meta = jnp.concatenate(
        [gate_weights.T, expert_ids.T.astype(F32), seg_ids.astype(F32), jnp.zeros((3, group), F32)], axis=0
    )
    vm = pl.BlockSpec(memory_space=pltpu.VMEM)
    hbm = pl.BlockSpec(memory_space=pl.ANY)
    dma = pltpu.SemaphoreType.DMA
    scratch = [
        pltpu.VMEM((group, width), BF16),
        pltpu.VMEM((dp, 8, group), F32),
        pltpu.VMEM((chunks, dp, group, sub), BF16),
        pltpu.VMEM((chunks, ex, dp - 1, cap, sub), BF16),
        pltpu.VMEM((chunks, dp, cap, depth), BF16),
        pltpu.VMEM((slots, depth, hidden), BF16),
        pltpu.VMEM((slots, depth, hidden), BF16),
        pltpu.VMEM((d_slots, w_down.shape[1], sub), BF16),
        pltpu.VMEM((dp * cap, hidden), F32),
        pltpu.VMEM((dp * cap, hidden), F32),
        pltpu.VMEM((tn, dp * cap, hidden), BF16),
        pltpu.VMEM((chunks, ex - 1, dp, cap, sub), BF16),
        pltpu.VMEM((chunks, dp, ex, cap, sub), BF16),
        pltpu.VMEM((chunks, dp - 1, group, sub), BF16),
        pltpu.VMEM((chunks, dp, group, sub), BF16),
        pltpu.VMEM((dp, group, ex * cap), BF16),
        pltpu.VMEM((group, LANES), F32),
        pltpu.VMEM((chunks, ex, count, sub), BF16),
        pltpu.VMEM((chunks, ex, count, sub), BF16),
        pltpu.VMEM((8, LANES), F32),
        pltpu.VMEM((ex * tn, 8, LANES), F32),
        dma((2, chunks)), dma((chunks * ex,)),
        dma((dp,)), dma((dp,)),
        dma((chunks, dp)), dma((chunks, dp)),
        dma((chunks, ex)), dma((chunks, ex)),
        dma((chunks, ex, tn)), dma((chunks, ex, tn)),
        dma((tn, n_h)), dma((tn, n_h)),
        dma((chunks, ex)), dma((chunks, ex)),
        dma((chunks, dp)), dma((chunks, dp)),
        dma((chunks, ex)), dma((chunks, ex)),
        dma((ex * tn,)), dma((ex * tn,)),
    ]
    layer_out, totals = pl.pallas_call(
        functools.partial(kernel, size),
        out_shape=(
            jax.ShapeDtypeStruct((count, half), BF16),
            jax.ShapeDtypeStruct((8, LANES), F32),
        ),
        in_specs=[vm, vm, vm, vm, hbm, hbm, hbm],
        out_specs=(vm, vm),
        scratch_shapes=scratch,
        compiler_params=pltpu.CompilerParams(
            collective_id=0, has_side_effects=True, vmem_limit_bytes=66_000_000
        ),
    )(tokens, norm_gain[None, :], meta, label_rows, w_gate, w_up, w_down)
    seq_totals = totals[0, :SEQS]
    slots_here = pair_slot[0]
    polarity = (1 - 2 * (slots_here % 2)).astype(F32)
    pair_member = (
        (slots_here // 2)[:, None] == jnp.arange(PAIRS, dtype=jnp.int32)[None, :]
    ).astype(F32)
    margins = dpo_beta * jnp.sum(
        pair_member * (polarity * (seq_totals - ref_scores[0]))[:, None], axis=0
    )
    return (layer_out, margins[None, :])


def solution(mesh):
    placed = (
        P("dp", None),
        P(),
        P("dp", None),
        P("dp", None),
        P("expert", None, ("dp", "tensor")),
        P("expert", None, ("dp", "tensor")),
        P("expert", "dp", "tensor"),
        P(("dp", "expert"), "tensor"),
        P("dp", None),
        P("dp", None),
        P("dp", None),
    )
    mesh_shape = tuple(mesh.shape[name] for name in ("dp", "expert", "tensor"))
    return jax.shard_map(
        functools.partial(body, mesh_shape),
        mesh=mesh,
        in_specs=placed,
        out_specs=(P(("dp", "expert"), "tensor"), P("dp", None)),
        check_vma=False,
    )
```
